128 devices in a mesh: grp: 4 (over x), row: 32 (over z, y, core).
Axes of the slice: x: 4, y: 4, z: 4, core: 2. Of those that a mesh axis runs over, the one named last changes fastest.
Arguments:
- vectors: bfloat16 [524288, 1024], P(('grp', 'row')), may hold values from -6 to 6
- keep_bits: int32 [524288], P(('grp', 'row')), may hold values 0 or 1
- counts: int32 [4096], P(('grp', 'row')), may hold values from 1 to 128
- block_list: int32 [4096], replicated, may hold values from 0 to 2047, as said below
- home_pos: int32 [2048], replicated, may hold values from 0 to 2047, as said below
- old_centroids: bfloat16 [2048, 1024], P('grp'), may hold values from -1.5 to 1.5
Outputs:
- new_centroids: bfloat16 [2048, 1024], P(('grp', 'row'))
- scores: float32 [524288, 512], P(('grp', 'row'))
The draws below stay inside these ranges and needn't reach their ends.
Inputs may be any that keep to these rules, and one draw needn't show every extreme that they name: `block_list`: every block's list is one of the lists of the block's own group; on one device at most one block has a list whose new position lies in any given other group, and this most is reached in every draw. `home_pos`: A permutation of the positions; position p lies in group p // 512.
All inputs are finite; a program needn't handle non-finite values. No bound on the sum of `keep_bits` on one device may be relied on, other than what follows from the above.
Results may differ from the reference program's by a relative error of at most 0.002.
Values may be sent and summed in bfloat16 or wider, within the bound.
A program may use at most 128 MiB of HBM per device.

```python
import math
import jax
import jax.numpy as jnp
from jax import lax

D = 1024
LISTS_GRP = 512
BLOCK = 128
PRIOR = 16
BLK_DEV = 32
BLOCKS = 4096
ROWS = 524288
LISTS = 2048
N_GRP = 4
N_ROW = 32


def draw_plan(key):
    base = jax.random.fold_in(key, 17)
    moved_per = LISTS_GRP // (2 * N_GRP)
    order_keys = jax.random.split(jax.random.fold_in(base, 1), N_GRP)
    orders = jax.vmap(lambda item: jax.random.permutation(item, LISTS_GRP))(order_keys).astype(jnp.int32)
    inverse = jnp.argsort(orders, axis=1, stable=True).astype(jnp.int32)
    group_ids = jnp.arange(N_GRP, dtype=jnp.int32)[:, None]
    slot_ids = jnp.arange(LISTS_GRP, dtype=jnp.int32)[None, :]
    leaves = orders < (N_GRP - 1) * moved_per
    direction = orders // moved_per
    within = orders % moved_per
    target = (group_ids + 1 + direction) % N_GRP
    back_dir = (group_ids - target - 1) % N_GRP
    wanted = jnp.clip(back_dir * moved_per + within, 0, LISTS_GRP - 1)
    target_safe = jnp.where(leaves, target, group_ids)
    new_slot = inverse[target_safe, wanted]
    homes = jnp.where(leaves, target * LISTS_GRP + new_slot, group_ids * LISTS_GRP + slot_ids)
    home_table = homes.reshape(-1).astype(jnp.int32)
    block_keys = jax.random.split(jax.random.fold_in(base, 2), N_GRP * N_ROW)
    perms = jax.vmap(lambda item: jax.random.permutation(item, BLK_DEV))(block_keys).astype(jnp.int32)
    place = jnp.argsort(perms, axis=1, stable=True).astype(jnp.int32).reshape(N_GRP, N_ROW, BLK_DEV)
    flags = jax.random.randint(jax.random.fold_in(base, 3), (N_GRP, N_ROW, BLK_DEV), 0, 2)
    forced_row = jax.random.randint(jax.random.fold_in(base, 4), (), 0, N_ROW)
    row_ids = jnp.arange(N_ROW, dtype=jnp.int32)[None, :, None]
    flags = jnp.where(row_ids == forced_row, 1, flags)
    moving = (place < N_GRP - 1) & (flags == 1)
    pick_move = jax.random.randint(jax.random.fold_in(base, 5), (N_GRP, N_ROW, BLK_DEV), 0, moved_per)
    stay_count = LISTS_GRP - (N_GRP - 1) * moved_per
    pick_stay = jax.random.randint(jax.random.fold_in(base, 6), (N_GRP, N_ROW, BLK_DEV), 0, stay_count)
    rank_wanted = jnp.where(moving, place * moved_per + pick_move, (N_GRP - 1) * moved_per + pick_stay)
    group_full = jnp.broadcast_to(jnp.arange(N_GRP, dtype=jnp.int32)[:, None, None], rank_wanted.shape)
    slots = inverse[group_full, rank_wanted]
    block_table = (group_full * LISTS_GRP + slots).reshape(-1).astype(jnp.int32)
    return (block_table, home_table)


def draw_block_list(key, part):
    return draw_plan(key)[0]


def draw_home_pos(key, part):
    return draw_plan(key)[1]


def with_ends(drawn, key, low, top_value):
    spot = [jax.random.randint(jax.random.fold_in(key, axis), (), 0, length) for axis, length in enumerate(drawn.shape)]
    longest = drawn.shape.index(max(drawn.shape))
    beside = spot[:longest] + [(spot[longest] + 1) % drawn.shape[longest]] + spot[longest + 1:]
    return drawn.at[tuple(spot)].set(low).at[tuple(beside)].set(top_value)


def levels(rng, shape, shards, low, high):
    factor_of, own = 1.0, jax.random.fold_in(rng, 6)
    for dim, shards_of in shards:
        steps = jnp.exp(jax.random.uniform(jax.random.fold_in(own, dim), (shards_of,), jnp.float32, low / len(shards), high / len(shards)))
        factor_of = factor_of * jnp.repeat(steps, shape[dim] // shards_of).reshape([-1 if axis == dim else 1 for axis in range(len(shape))])
    return factor_of


def noise(key, shape, width, limit, pieces=(), held_as=jnp.bfloat16):
    loudness = levels(key, shape, pieces, -0.22, 0.18) if pieces else 1.0
    entries = jax.random.normal(key, shape, jnp.float32) * width * loudness
    return jnp.minimum(jnp.maximum(entries, -limit), limit).astype(held_as)


def setup_inputs(seed: int = 0) -> dict:
    streams_of = jax.random.split(jax.random.key(seed), 7)
    vectors = noise(streams_of[0], (ROWS, D), 1.0, 6.0, ((0, 128),))
    keep_bits = with_ends((jax.random.randint(streams_of[1], (ROWS,), 0, 2) < 1).astype(jnp.int32), jax.random.fold_in(streams_of[1], 1), 0, 1)
    counts = with_ends(jax.random.randint(streams_of[2], (BLOCKS,), 1, BLOCK + 1), jax.random.fold_in(streams_of[2], 1), 1, BLOCK).astype(jnp.int32)
    block_list = draw_block_list(jax.random.fold_in(streams_of[6], 71), 0)
    home_pos = draw_home_pos(jax.random.fold_in(streams_of[6], 71), 0)
    old_centroids = noise(streams_of[5], (LISTS, D), 0.25, 1.5, ((0, 4),))
    return dict(vectors=vectors, keep_bits=keep_bits, counts=counts, block_list=block_list, home_pos=home_pos, old_centroids=old_centroids)


def centroid_rows(sums, totals, previous):
    prior_weight = 1.0 * PRIOR
    return ((sums + prior_weight * previous.astype(jnp.float32)) / (totals + prior_weight)[:, None]).astype(jnp.bfloat16)

def reference(vectors, keep_bits, counts, block_list, home_pos, old_centroids):
    blocks = counts.shape[0]
    row_blocks = vectors.reshape(blocks, BLOCK, D)
    position = jnp.arange(BLOCK, dtype=jnp.int32)[None, :]
    alive = (keep_bits.reshape(blocks, BLOCK) * (position < counts[:, None]).astype(jnp.int32)).astype(jnp.float32)

    def block_sum(item):
        rows, weights = item
        return jnp.dot(weights.astype(jnp.bfloat16), rows, preferred_element_type=jnp.float32)
    block_sums = lax.map(block_sum, (row_blocks, alive))
    block_counts = lax.optimization_barrier(jnp.sum(alive, axis=1))
    homes = jnp.take(home_pos, block_list).astype(jnp.int32)
    sums = jax.ops.segment_sum(block_sums, homes, num_segments=LISTS)
    totals = jax.ops.segment_sum(block_counts, homes, num_segments=LISTS)
    table = centroid_rows(sums, totals, old_centroids)
    norms = lax.optimization_barrier(jnp.sum(jnp.square(table.astype(jnp.float32)), axis=1))
    home_groups = (homes // LISTS_GRP).astype(jnp.int32)
    factor = 1.0 / math.sqrt(D)

    def block_scores(item):
        rows, weights, group_of = item
        start = (group_of * LISTS_GRP).astype(jnp.int32)
        part = lax.dynamic_slice_in_dim(table, start, LISTS_GRP, 0)
        part_norms = lax.dynamic_slice_in_dim(norms, start, LISTS_GRP, 0)
        dots = lax.dot_general(rows, part, (((1,), (1,)), ((), ())), preferred_element_type=jnp.float32)
        return (2.0 * dots - part_norms[None, :]) * factor * weights[:, None]
    scores = lax.map(block_scores, (row_blocks, alive, home_groups))
    return (table, scores.reshape(blocks * BLOCK, LISTS_GRP))
```

```python
import functools
import math

import jax
import jax.numpy as jnp
from jax import lax
from jax.experimental import pallas as pl
from jax.experimental.pallas import tpu as pltpu
from jax.sharding import PartitionSpec as P

PRIOR = 16
MESH = pl.DeviceIdType.MESH
LANES = 128
NT = (((1,), (1,)), ((), ()))


def iota(shape, dim):
    return lax.broadcasted_iota(jnp.int32, shape, dim)


def sums_kernel(bl, hp, cnt, keep_ref, vec_ref, vec_hbm, msg_ref, xmsg_ref, fr_ref, pick_ref,
                sums, alive, sems, *, blocks, lists_group, n_groups, n_rows):
    step = pl.program_id(0)
    steps = pl.num_programs(0)
    g = lax.axis_index("grp")
    d = lax.axis_index("row")
    base = (g * n_rows + d) * blocks

    def fetch(j):
        first = pl.multiple_of(pick_ref[4 + j] * LANES, LANES)
        return pltpu.make_async_copy(vec_hbm.at[pl.ds(first, LANES), :], fr_ref.at[j], sems.at[j])

    @pl.when(step == 0)
    def _():
        rows = iota((blocks, LANES), 0)
        limit = jnp.zeros((blocks, LANES), jnp.int32)
        picks = [jnp.int32(-1)] * (n_groups - 1)
        for k in range(blocks):
            limit = jnp.where(rows == k, cnt[k], limit)
            home = hp[bl[base + k]]
            away = lax.rem(home // lists_group - g + n_groups, n_groups)
            picks = [jnp.where(away == j + 1, k, pick) for j, pick in enumerate(picks)]
        alive[...] = jnp.where(iota((blocks, LANES), 1) < limit, keep_ref[...], 0).astype(jnp.float32)
        for j, pick in enumerate(picks):
            pick_ref[j] = pick
            pick_ref[4 + j] = jnp.maximum(pick, 0)
            fetch(j).start()

    rows8 = iota((8, LANES), 0)
    mine = alive[pl.ds(pl.multiple_of(step * 8, 8), 8), :]
    weights = jnp.concatenate(
        [jnp.where(rows8 == j, mine, 0.0).astype(jnp.bfloat16) for j in range(8)], axis=1
    )
    sums[pl.ds(pl.multiple_of(step * 8, 8), 8), :] = jnp.dot(
        weights, vec_ref[...], preferred_element_type=jnp.float32
    )

    @pl.when(step == steps - 1)
    def _():
        lane8 = iota((8, LANES), 1)
        first = lax.rem(d, 4) * blocks
        slots = jnp.zeros((8, LANES), jnp.int32)
        here = rows8 == d // 4
        for k in range(blocks):
            home = hp[bl[base + k]]
            slot = jnp.where(home // lists_group == g, lax.rem(home, lists_group) + 1, 0)
            slots = jnp.where(lane8 == first + k, slot, slots)
        counts = jnp.sum(alive[...], axis=1, keepdims=True)
        placed = jnp.where(iota((blocks, LANES), 1) == first + iota((blocks, LANES), 0), counts, 0.0)
        counts_row = jnp.sum(placed, axis=0, keepdims=True)
        code = jnp.where(here & (slots > 0), slots.astype(jnp.float32) * 256.0 + counts_row, 0.0)
        slabs = sums.shape[1] // LANES
        for s in range(slabs):
            msg_ref[s, 0:blocks, :] = sums[:, s * LANES:(s + 1) * LANES]
            msg_ref[s, blocks:blocks + 8, :] = code
        for j in range(n_groups - 1):
            pick = pick_ref[4 + j]
            valid = jnp.where(pick_ref[j] >= 0, 1.0, 0.0).astype(jnp.float32)
            row = sums[pl.ds(pick, 1), :] * valid
            count = jnp.sum(alive[pl.ds(pick, 1), :], axis=1, keepdims=True)
            slot = lax.rem(hp[bl[base + pick]], lists_group) + 1
            value = (slot.astype(jnp.float32) * 256.0 + count) * valid
            at = (rows8 == 3 + d // 16) & (lane8 == 8 * lax.rem(d, 16) + j)
            for s in range(slabs):
                xmsg_ref[j, s] = jnp.where(
                    rows8 == j, row[:, s * LANES:(s + 1) * LANES], jnp.where(at, value, 0.0)
                )
            fetch(j).wait()


def gather_kernel(msg, xmsg, fr, old, table_out, norms_out, fs_out,
                  g1, a1, xin, arr, g2, a2, frin, tab,
                  s1s, s1r, s1b_s, s1b_r, xs, xr, fs_s, fs_r, s2s, s2r, s2b_s, s2b_r,
                  s3s, s3r, rs, rr, ls, *, blocks, n_groups, factor):
    g = lax.axis_index("grp")
    d = lax.axis_index("row")
    core = lax.rem(d, 2)
    y = lax.rem(d // 2, 4)
    z = d // 8
    flat = core == 0
    u = jnp.where(flat, y, z)
    v = jnp.where(flat, z, y)
    sid = core * 4 + u
    partner = d + 1 - 2 * core

    def row_of(zz, yy, cc):
        return (zz * 4 + yy) * 2 + cc

    def along_u(i):
        w = lax.rem(u + i, 4)
        return jnp.where(flat, row_of(z, w, core), row_of(w, y, core))

    def along_v(i):
        w = lax.rem(v + i, 4)
        return jnp.where(flat, row_of(w, y, core), row_of(z, w, core))

    def copy(src, dst, send, recv, where):
        return pltpu.make_async_remote_copy(
            src_ref=src, dst_ref=dst, send_sem=send, recv_sem=recv,
            device_id=where, device_id_type=MESH,
        )

    barrier = pltpu.get_barrier_semaphore()
    greeted = 0
    for i in range(1, 4):
        for c in range(2):
            pl.semaphore_signal(barrier, inc=1, device_id={"row": row_of(z, lax.rem(y + i, 4), c)},
                                device_id_type=MESH)
            pl.semaphore_signal(barrier, inc=1, device_id={"row": row_of(lax.rem(z + i, 4), y, c)},
                                device_id_type=MESH)
            greeted += 2
        pl.semaphore_signal(barrier, inc=1, device_id={"grp": lax.rem(g + i, n_groups)},
                            device_id_type=MESH)
        greeted += 1
    pl.semaphore_signal(barrier, inc=1, device_id={"row": partner}, device_id_type=MESH)
    pl.semaphore_wait(barrier, greeted + 1)

    xcopies = []
    for i in range(1, n_groups):
        where = {"grp": lax.rem(g + i, n_groups)}
        xcopies.append(copy(xmsg.at[i - 1], xin.at[i - 1], xs.at[i - 1], xr.at[i - 1], where))
        xcopies[-1].start()

    def slab_sends(src, dst, send, recv):
        out = []
        for i in range(1, 4):
            yy = lax.rem(y + i, 4)
            q = y * 2 + core
            out.append(copy(src.at[yy], dst.at[q], send.at[2 * i], recv.at[q],
                            {"row": row_of(z, yy, 0)}))
            zz = lax.rem(z + i, 4)
            q = z * 2 + core
            out.append(copy(src.at[4 + zz], dst.at[q], send.at[2 * i + 1], recv.at[q],
                            {"row": row_of(zz, y, 1)}))
        theirs = jnp.where(flat, 4 + z, y)
        q = jnp.where(flat, z, y) * 2 + core
        out.append(copy(src.at[theirs], dst.at[q], send.at[1], recv.at[q], {"row": partner}))
        for item in out:
            item.start()
        own = u * 2 + core
        local = pltpu.make_async_copy(src.at[sid], dst.at[own], recv.at[own])
        local.start()
        return out, local

    def slab_waits(started, src, dst, send, recv):
        out, local = started
        local.wait()
        own = u * 2 + core
        for i in range(1, 8):
            q = lax.rem(own + i, 8)
            copy(src.at[0], dst.at[q], send.at[0], recv.at[q], {"row": partner}).wait_recv()
        for item in out:
            item.wait_send()

    first = slab_sends(msg, g1, s1s, s1r)

    fcopies = []
    for i in range(1, n_groups):
        where = {"grp": lax.rem(g + i, n_groups)}
        fcopies.append(copy(fr.at[i - 1], frin.at[i - 1], fs_s.at[i - 1], fs_r.at[i - 1], where))

    for item in xcopies:
        item.wait()
    for item in fcopies:
        item.start()
    for s in range(8):
        arr[s] = xin[0, s] + xin[1, s] + xin[2, s]
    slab_waits(first, msg, g1, s1s, s1r)

    def plane_sends(src, dst, send, recv):
        out = []
        for i in range(1, 4):
            out.append(copy(src, dst.at[v], send.at[i], recv.at[i], {"row": along_v(i)}))
            out[-1].start()
        local = pltpu.make_async_copy(src, dst.at[v], recv.at[0])
        local.start()
        return out, local

    def plane_waits(started):
        out, local = started
        local.wait()
        for item in out:
            item.wait()

    plane = plane_sends(g1, g2, s2s, s2r)
    second = slab_sends(arr, a1, s1b_s, s1b_r)
    slab_waits(second, arr, a1, s1b_s, s1b_r)
    plane_b = plane_sends(a1, a2, s2b_s, s2b_r)
    plane_waits(plane)

    lists = tab.shape[0]
    codes = jnp.zeros((8, LANES), jnp.float32)
    for i in range(4):
        for q in range(8):
            codes = codes + g2[i, q, blocks:blocks + 8, :]
    codes = codes.astype(jnp.int32)
    target = iota((lists, LANES), 0)

    def piece(ref, zz, yy, count):
        one = jnp.where(flat, zz, yy)
        two = jnp.where(flat, yy, zz) * 2
        return [ref[one, two, 0:count, :], ref[one, two + 1, 0:count, :]]

    def split(values):
        high = values.astype(jnp.bfloat16)
        low = (values - high.astype(jnp.float32)).astype(jnp.bfloat16)
        return jnp.concatenate([high, low], axis=1)

    def chunk(rows, values):
        slots = [(row >> 8) - 1 for row in rows]
        held = [(row & 255).astype(jnp.float32) for row in rows]
        hot = jnp.concatenate(
            [jnp.where(target == slot, 1.0, 0.0).astype(jnp.bfloat16) for slot in slots], axis=1
        )
        part = jnp.dot(hot, split(values), preferred_element_type=jnp.float32)
        held = jnp.concatenate(held, axis=1)
        held = jnp.broadcast_to(held, (LANES, held.shape[1])).astype(jnp.bfloat16)
        total = lax.dot_general(hot, held, NT, preferred_element_type=jnp.float32)
        return part[:, :LANES] + part[:, LANES:], total

    sums = jnp.zeros((lists, LANES), jnp.float32)
    totals = jnp.zeros((lists, LANES), jnp.float32)
    for zz in range(4):
        values = jnp.concatenate(sum([piece(g2, zz, yy, blocks) for yy in range(4)], []), axis=0)
        part, total = chunk([codes[2 * zz:2 * zz + 1], codes[2 * zz + 1:2 * zz + 2]], values)
        sums, totals = sums + part, totals + total
    plane_waits(plane_b)
    codes = jnp.zeros((8, LANES), jnp.float32)
    for i in range(4):
        for q in range(8):
            codes = codes + a2[i, q]
    codes = codes[3:5].astype(jnp.int32)
    values = jnp.concatenate(
        sum([piece(a2, zz, yy, 8) for zz in range(4) for yy in range(4)], []), axis=0
    )
    part, total = chunk([codes[0:1], codes[1:2]], values)
    sums, totals = sums + part, totals + total

    def columns(s):
        return pl.ds(pl.multiple_of(s * LANES, LANES), LANES)

    previous = old[:, columns(sid)].astype(jnp.float32)
    prior = 1.0 * PRIOR
    tab[:, columns(sid)] = ((sums + prior * previous) / (totals + prior)).astype(jnp.bfloat16)

    spread = []
    for i in range(1, 4):
        ref = tab.at[:, columns(sid)]
        spread.append(copy(ref, ref, s3s.at[i], s3r.at[i], {"row": along_u(i)}))
        spread[-1].start()
    ref = tab.at[:, columns(sid)]
    relays = [copy(ref, ref, rs.at[0], rr.at[0], {"row": partner})]
    relays[0].start()
    for i in range(1, 4):
        ref = tab.at[:, columns(core * 4 + lax.rem(u - i + 4, 4))]
        copy(ref, ref, s3s.at[i], s3r.at[i], {"row": partner}).wait_recv()
        relays.append(copy(ref, ref, rs.at[i], rr.at[i], {"row": partner}))
        relays[-1].start()
    for i in range(4):
        w = jnp.where(flat, z, y)
        ref = tab.at[:, columns((1 - core) * 4 + lax.rem(w - i + 4, 4))]
        copy(ref, ref, rs.at[i], rr.at[i], {"row": partner}).wait_recv()
    out = pltpu.make_async_copy(tab, table_out, ls.at[0])
    out.start()

    ones = jnp.ones((8, tab.shape[1]), jnp.bfloat16)
    squares = jnp.square(tab[...].astype(jnp.float32))
    high = squares.astype(jnp.bfloat16)
    low = (squares - high.astype(jnp.float32)).astype(jnp.bfloat16)
    norms = lax.dot_general(ones, high, NT, preferred_element_type=jnp.float32)
    norms = norms + lax.dot_general(ones, low, NT, preferred_element_type=jnp.float32)
    norms_out[...] = norms
    for item in fcopies:
        item.wait()
    for j in range(n_groups - 1):
        dots = lax.dot_general(frin[j], tab[...], NT, preferred_element_type=jnp.float32)
        fs_out[j] = ((2.0 * dots - norms[0:1]) * factor).astype(jnp.bfloat16)
    for item in spread:
        item.wait_send()
    for item in relays:
        item.wait_send()
    out.wait()


def alive_column(row):
    eye = iota((LANES, LANES), 0) == iota((LANES, LANES), 1)
    return jnp.sum(jnp.where(eye, row, 0.0), axis=1, keepdims=True)


def scores_kernel(cnt, keep_ref, vec_ref, table, norms, scores_ref, new_ref, *, factor, share):
    step = pl.program_id(0)
    d = lax.axis_index("row")

    @pl.when(step == 0)
    def _():
        new_ref[...] = table[pl.ds(pl.multiple_of(d * share, share), share), :]

    n = vec_ref.shape[0] // LANES
    lane = iota((1, LANES), 1)
    dots = lax.dot_general(vec_ref[...], table[...], NT, preferred_element_type=jnp.float32)
    for b in range(n):
        k = step * n + b
        row = jnp.where(lane < cnt[k], keep_ref[pl.ds(k, 1), :], 0).astype(jnp.float32)
        scores_ref[b * LANES:(b + 1) * LANES, :] = (
            (2.0 * dots[b * LANES:(b + 1) * LANES] - norms[0:1]) * factor
        ) * alive_column(row)


def merge_kernel(pick, cnt, keep_ref, b0, b1, b2, _, scores_ref, held, sems):
    lane = iota((1, LANES), 1)
    backs = (b0, b1, b2)

    def put(j):
        first = pl.multiple_of(pick[4 + j] * LANES, LANES)
        return pltpu.make_async_copy(held.at[j], scores_ref.at[pl.ds(first, LANES), :], sems.at[j])

    for j, back in enumerate(backs):
        @pl.when(pick[j] >= 0)
        def _():
            k = pick[4 + j]
            row = jnp.where(lane < cnt[k], keep_ref[pl.ds(k, 1), :], 0).astype(jnp.float32)
            held[j] = back[...].astype(jnp.float32) * alive_column(row)
            put(j).start()
    for j in range(len(backs)):
        @pl.when(pick[j] >= 0)
        def _():
            put(j).wait()


def local(vectors, keep_bits, counts, block_list, home_pos, old_centroids):
    n_groups = lax.axis_size("grp")
    n_rows = lax.axis_size("row")
    blocks = counts.shape[0]
    total_rows, width = vectors.shape
    block_rows = total_rows // blocks
    lists_group = old_centroids.shape[0]
    factor = 1.0 / math.sqrt(width)
    slabs = width // LANES
    away = n_groups - 1
    keep = keep_bits.reshape(blocks, block_rows)
    whole = pl.BlockSpec(memory_space=pltpu.VMEM)
    f32, bf16 = jnp.float32, jnp.bfloat16

    def full(*shape):
        return pl.BlockSpec(shape, lambda *_: (0,) * len(shape))

    rows = 8 * block_rows
    msg, xmsg, leaving, picks = pl.pallas_call(
        functools.partial(sums_kernel, blocks=blocks, lists_group=lists_group,
                          n_groups=n_groups, n_rows=n_rows),
        out_shape=(
            jax.ShapeDtypeStruct((slabs, blocks + 8, LANES), f32),
            jax.ShapeDtypeStruct((away, slabs, 8, LANES), f32),
            jax.ShapeDtypeStruct((away, block_rows, width), bf16),
            jax.ShapeDtypeStruct((8,), jnp.int32),
        ),
        grid_spec=pltpu.PrefetchScalarGridSpec(
            num_scalar_prefetch=3,
            grid=(total_rows // rows,),
            in_specs=[
                full(blocks, block_rows),
                pl.BlockSpec((rows, width), lambda i, *_: (i, 0)),
                pl.BlockSpec(memory_space=pl.ANY),
            ],
            out_specs=(
                full(slabs, blocks + 8, LANES),
                full(away, slabs, 8, LANES),
                full(away, block_rows, width),
                pl.BlockSpec(memory_space=pltpu.SMEM),
            ),
            scratch_shapes=[
                pltpu.VMEM((blocks, width), f32),
                pltpu.VMEM((blocks, LANES), f32),
                pltpu.SemaphoreType.DMA((away,)),
            ],
        ),
        name="block_sums",
    )(block_list, home_pos, counts, keep, vectors, vectors)

    dma = pltpu.SemaphoreType.DMA
    table, norms, found = pl.pallas_call(
        functools.partial(gather_kernel, blocks=blocks, n_groups=n_groups, factor=factor),
        out_shape=(
            jax.ShapeDtypeStruct((lists_group, width), bf16),
            jax.ShapeDtypeStruct((8, lists_group), f32),
            jax.ShapeDtypeStruct((away, block_rows, lists_group), bf16),
        ),
        in_specs=[whole] * 4,
        out_specs=(pl.BlockSpec(memory_space=pl.ANY), whole, whole),
        scratch_shapes=[
            pltpu.VMEM((8, blocks + 8, LANES), f32),
            pltpu.VMEM((8, 8, LANES), f32),
            pltpu.VMEM((away, slabs, 8, LANES), f32),
            pltpu.VMEM((slabs, 8, LANES), f32),
            pltpu.VMEM((4, 8, blocks + 8, LANES), f32),
            pltpu.VMEM((4, 8, 8, LANES), f32),
            pltpu.VMEM((away, block_rows, width), bf16),
            pltpu.VMEM((lists_group, width), bf16),
            dma((8,)), dma((8,)), dma((8,)), dma((8,)),
            dma((4,)), dma((4,)), dma((4,)), dma((4,)),
            dma((4,)), dma((4,)), dma((4,)), dma((4,)),
            dma((4,)), dma((4,)), dma((4,)), dma((4,)),
            dma((1,)),
        ],
        compiler_params=pltpu.CompilerParams(collective_id=0, has_side_effects=True),
        name="table_exchange",
    )(msg, xmsg, leaving, old_centroids)

    backs = [
        lax.ppermute(found[j], "grp", [(s, (s - j - 1) % n_groups) for s in range(n_groups)])
        for j in range(away)
    ]

    rows = 4 * block_rows
    scores, new_centroids = pl.pallas_call(
        functools.partial(scores_kernel, factor=factor, share=lists_group // n_rows),
        out_shape=(
            jax.ShapeDtypeStruct((total_rows, lists_group), f32),
            jax.ShapeDtypeStruct((lists_group // n_rows, width), bf16),
        ),
        grid_spec=pltpu.PrefetchScalarGridSpec(
            num_scalar_prefetch=1,
            grid=(total_rows // rows,),
            in_specs=[
                full(blocks, block_rows),
                pl.BlockSpec((rows, width), lambda i, *_: (i, 0)),
                full(lists_group, width),
                full(8, lists_group),
            ],
            out_specs=(
                pl.BlockSpec((rows, lists_group), lambda i, *_: (i, 0)),
                full(lists_group // n_rows, width),
            ),
        ),
        cost_estimate=pl.CostEstimate(
            flops=2 * total_rows * width * lists_group,
            bytes_accessed=total_rows * (2 * width + 4 * lists_group),
            transcendentals=0,
        ),
        name="scores",
    )(counts, keep, vectors, table, norms)

    scores = pl.pallas_call(
        merge_kernel,
        out_shape=jax.ShapeDtypeStruct(scores.shape, f32),
        grid_spec=pltpu.PrefetchScalarGridSpec(
            num_scalar_prefetch=2,
            grid=(1,),
            in_specs=[full(blocks, block_rows)] + [full(block_rows, lists_group)] * away
            + [pl.BlockSpec(memory_space=pl.ANY)],
            out_specs=pl.BlockSpec(memory_space=pl.ANY),
            scratch_shapes=[
                pltpu.VMEM((away, block_rows, lists_group), f32),
                pltpu.SemaphoreType.DMA((away,)),
            ],
        ),
        input_output_aliases={6: 0},
        name="merge",
    )(picks, counts, keep, *backs, scores)
    return new_centroids, scores


def solution(mesh):
    in_specs = (
        P(("grp", "row"), None),
        P(("grp", "row")),
        P(("grp", "row")),
        P(),
        P(),
        P("grp", None),
    )
    out_specs = (P(("grp", "row"), None), P(("grp", "row"), None))
    return jax.shard_map(local, mesh=mesh, in_specs=in_specs, out_specs=out_specs, check_vma=False)
```

```python
import functools
import math

import jax
import jax.numpy as jnp
from jax import lax
from jax.experimental import pallas as pl
from jax.experimental.pallas import tpu as pltpu
from jax.sharding import PartitionSpec as P

PRIOR = 16
MESH = pl.DeviceIdType.MESH
LANES = 128
NT = (((1,), (1,)), ((), ()))


def iota(shape, dim):
    return lax.broadcasted_iota(jnp.int32, shape, dim)


def table_kernel(bl_hbm, hp_hbm, cnt_hbm, keep_hbm, vec_hbm, old_hbm,
                 vec, table, norms_out, f0, f1, f2,
                 bl, hp, cnt, keep, alive, sums, msg, xmsg, leaving, previous,
                 xin, arr, g2, a2, passing, arrived,
                 load_sem, small_sem, p1_s, p1_r, p1b_s, p1b_r, x_s, x_r, bulk_s, bulk_r,
                 p2_s, p2_r, p2b_s, p2b_r, p3_s, p3_r, mate_s, mate_r,
                 *, n_groups, n_rows, factor):
    blocks = alive.shape[0]
    slabs = msg.shape[0]
    g = lax.axis_index("grp")
    d = lax.axis_index("row")
    core = lax.rem(d, 2)
    y = lax.rem(d // 2, 4)
    z = d // 8
    flat = core == 0
    u = jnp.where(flat, y, z)
    v = jnp.where(flat, z, y)
    sid = core * 4 + u
    partner = d + 1 - 2 * core
    mate = {"row": partner}
    base = (g * n_rows + d) * blocks
    rows8 = iota((8, LANES), 0)
    lane8 = iota((8, LANES), 1)

    def row_of(zz, yy, cc):
        return (zz * 4 + yy) * 2 + cc

    def along_u(i):
        w = lax.rem(u + i, 4)
        return {"row": jnp.where(flat, row_of(z, w, core), row_of(w, y, core))}

    def along_v(i):
        w = lax.rem(v + i, 4)
        return {"row": jnp.where(flat, row_of(w, y, core), row_of(z, w, core))}

    def group(i):
        return {"grp": lax.rem(g + i, n_groups)}

    def copy(src, dst, send, recv, where):
        return pltpu.make_async_remote_copy(
            src_ref=src, dst_ref=dst, send_sem=send, recv_sem=recv,
            device_id=where, device_id_type=MESH,
        )

    def columns(s):
        return pl.ds(pl.multiple_of(s * LANES, LANES), LANES)

    small = [
        pltpu.make_async_copy(src, dst, small_sem.at[i])
        for i, (src, dst) in enumerate(((bl_hbm, bl), (hp_hbm, hp), (cnt_hbm, cnt), (keep_hbm, keep)))
    ]
    for item in small:
        item.start()
    chunks = load_sem.shape[0]
    size = vec.shape[0] // chunks
    loads = [
        pltpu.make_async_copy(
            vec_hbm.at[pl.ds(i * size, size), :], vec.at[pl.ds(i * size, size), :], load_sem.at[i]
        )
        for i in range(chunks)
    ]
    for item in loads:
        item.start()
    prior_load = pltpu.make_async_copy(old_hbm.at[:, columns(sid)], previous, small_sem.at[4])
    prior_load.start()

    barrier = pltpu.get_barrier_semaphore()
    peers = [mate]
    for i in range(1, 4):
        for c in range(2):
            peers.append({"row": row_of(z, lax.rem(y + i, 4), c)})
            peers.append({"row": row_of(lax.rem(z + i, 4), y, c)})
    for i in range(1, n_groups):
        peers.append(group(i))
    for where in peers:
        pl.semaphore_signal(barrier, inc=1, device_id=where, device_id_type=MESH)

    for item in small:
        item.wait()
    rows = iota((blocks, LANES), 0)
    lanes = iota((blocks, LANES), 1)
    lane = iota((1, LANES), 1)
    eye = iota((blocks, blocks), 0) == iota((blocks, blocks), 1)
    limit = jnp.sum(jnp.where(eye, cnt[...], 0), axis=1, keepdims=True)
    alive[...] = jnp.where(lanes < limit, keep[...], 0).astype(jnp.float32)
    first = lax.rem(d, 4) * blocks
    counts = jnp.sum(alive[...], axis=1, keepdims=True)
    counts_row = jnp.sum(jnp.where(lanes == first + rows, counts, 0.0), axis=0, keepdims=True)

    lists = table.shape[0]
    per_group = lists // LANES
    homes = jnp.concatenate([hp[pl.ds(g * per_group + i, 1), :] for i in range(per_group)], axis=1)
    line = iota((8, lists), 0)
    digits = jnp.where(line == 0, homes >> 8, jnp.where(line == 1, homes & 255, 0))
    listed = bl[pl.ds(g * (n_rows * blocks // LANES) + d // 4, 1), :] - g * lists
    hot = jnp.where(iota((lists, LANES), 0) == listed, 1.0, 0.0).astype(jnp.bfloat16)
    found = jnp.dot(
        digits.astype(jnp.float32).astype(jnp.bfloat16), hot, preferred_element_type=jnp.float32
    ).astype(jnp.int32)
    home = found[0:1] * 256 + found[1:2]
    slot = lax.rem(home, lists)
    away = lax.rem(home // lists - g + n_groups, n_groups)
    own_lanes = (lane >= first) & (lane < first + blocks)
    worth = (slot + 1).astype(jnp.float32) * 256.0 + counts_row
    staying = jnp.where(own_lanes & (away == 0), worth, 0.0)
    code = jnp.where(rows8 == d // 4, staying, 0.0)
    for s in range(slabs):
        msg[s, blocks:blocks + 8, :] = code
    values, marks = [], []
    for j in range(n_groups - 1):
        going = jnp.where(own_lanes & (away == j + 1), 1.0, 0.0)
        values.append(jnp.sum(going * worth, axis=1, keepdims=True))
        marks.append(jnp.sum(jnp.where(lanes == first + rows, going, 0.0), axis=1, keepdims=True))

    def keep_leaving(i):
        for j, mark in enumerate(marks):
            part = jnp.zeros((LANES, vec.shape[1]), jnp.bfloat16)
            for k in range(i * 8, i * 8 + 8):
                weight = mark[k:k + 1].astype(jnp.bfloat16)
                part = part + vec[k * LANES:(k + 1) * LANES, :] * weight
            leaving[j] = part if i == 0 else leaving[j] + part

    per = chunks * 8 // blocks
    for i in range(blocks // 8):
        for item in loads[i * per:(i + 1) * per]:
            item.wait()
        mine = alive[i * 8:(i + 1) * 8, :]
        weights = jnp.concatenate(
            [jnp.where(rows8 == j, mine, 0.0).astype(jnp.bfloat16) for j in range(8)], axis=1
        )
        part = jnp.dot(
            weights, vec[i * 8 * LANES:(i + 1) * 8 * LANES, :], preferred_element_type=jnp.float32
        )
        sums[i * 8:(i + 1) * 8, :] = part
        for s in range(slabs):
            msg[s, i * 8:(i + 1) * 8, :] = part[:, s * LANES:(s + 1) * LANES]
        if i < blocks // 8 - 1:
            keep_leaving(i)

    pl.semaphore_wait(barrier, len(peers))

    def slab_sends(src, dst, send, recv):
        out = []
        for i in range(1, 4):
            yy = lax.rem(y + i, 4)
            q = y * 2 + core
            out.append(copy(src.at[yy], dst.at[z, q], send.at[2 * i], recv.at[q],
                            {"row": row_of(z, yy, 0)}))
            zz = lax.rem(z + i, 4)
            q = z * 2 + core
            out.append(copy(src.at[4 + zz], dst.at[y, q], send.at[2 * i + 1], recv.at[q],
                            {"row": row_of(zz, y, 1)}))
        theirs = jnp.where(flat, 4 + z, y)
        q = jnp.where(flat, z, y) * 2 + core
        out.append(copy(src.at[theirs], dst.at[jnp.where(flat, y, z), q], send.at[1], recv.at[q], mate))
        for item in out:
            item.start()
        own = u * 2 + core
        kept = pltpu.make_async_copy(src.at[sid], dst.at[v, own], recv.at[own])
        kept.start()
        return out, kept

    def slab_waits(started, src, dst, send, recv):
        out, kept = started
        kept.wait()
        own = u * 2 + core
        for i in range(1, 8):
            q = lax.rem(own + i, 8)
            copy(src.at[0], dst.at[v, q], send.at[0], recv.at[q], mate).wait_recv()
        for item in out:
            item.wait_send()

    def ring_start(near, at, part, send, recv):
        right, left = near(1), near(3)
        out = [
            copy(part(at, h), part(at, h), send.at[n], recv.at[n], to)
            for n, (h, to) in enumerate(((0, right), (1, left), (1, right), (0, left)))
        ]
        for item in out:
            item.start()
        return out

    def ring_wait(near, at, part, send, recv, n):
        frm = (3, 1, 3, 1, 2, 2)[n]
        ref = part(lax.rem(at + frm, 4), (0, 1, 1, 0, 0, 1)[n])
        copy(ref, ref, send.at[n], recv.at[n], near(1)).wait_recv()

    def ring_relay(near, at, part, send, recv):
        out = []
        for n, (frm, h, to) in enumerate(((3, 0, 1), (1, 1, 3))):
            ring_wait(near, at, part, send, recv, n)
            ref = part(lax.rem(at + frm, 4), h)
            out.append(copy(ref, ref, send.at[4 + n], recv.at[4 + n], near(to)))
            out[-1].start()
        return out

    first_sent = slab_sends(msg, g2, p1_s, p1_r)
    for j in range(n_groups - 1):
        row = jnp.sum(sums[...] * marks[j], axis=0, keepdims=True)
        at = (rows8 == 3 + d // 16) & (lane8 == 8 * lax.rem(d, 16) + j)
        for s in range(slabs):
            xmsg[j, s] = jnp.where(
                rows8 == j, row[:, s * LANES:(s + 1) * LANES], jnp.where(at, values[j], 0.0)
            )
    xcopies = [
        copy(xmsg.at[i - 1], xin.at[i - 1], x_s.at[i - 1], x_r.at[i - 1], group(i))
        for i in range(1, n_groups)
    ]
    for item in xcopies:
        item.start()

    keep_leaving(blocks // 8 - 1)
    half = LANES // 2
    low, high = pl.ds(0, half), pl.ds(half, half)
    bulk = [
        copy(leaving.at[1, low], passing.at[0], bulk_s.at[0], bulk_r.at[0], group(1)),
        copy(leaving.at[1, high], passing.at[1], bulk_s.at[1], bulk_r.at[1], group(3)),
        copy(leaving.at[0], arrived.at[0], bulk_s.at[2], bulk_r.at[2], group(1)),
        copy(leaving.at[2], arrived.at[2], bulk_s.at[3], bulk_r.at[3], group(3)),
    ]
    bulk_on = [
        copy(passing.at[0], arrived.at[1, low], bulk_s.at[4], bulk_r.at[4], group(1)),
        copy(passing.at[1], arrived.at[1, high], bulk_s.at[5], bulk_r.at[5], group(3)),
    ]
    for item in xcopies:
        item.wait()
    for item in bulk:
        item.start()
    for s in range(slabs):
        arr[s] = xin[0, s] + xin[1, s] + xin[2, s]
    slab_waits(first_sent, msg, g2, p1_s, p1_r)

    def plane(at, h):
        return g2.at[at, pl.ds(4 * h, 4)]

    def plane_b(at, h):
        return a2.at[at, pl.ds(4 * h, 4)]

    p2 = (along_v, v, plane, p2_s, p2_r)
    p2b = (along_v, v, plane_b, p2b_s, p2b_r)
    sent = ring_start(*p2)
    second_sent = slab_sends(arr, a2, p1b_s, p1b_r)
    slab_waits(second_sent, arr, a2, p1b_s, p1b_r)
    sent_b = ring_start(*p2b)
    sent += ring_relay(*p2)
    sent_b += ring_relay(*p2b)
    for n in range(2):
        bulk[n].wait_recv()
        bulk_on[n].start()
    for n in range(2, 6):
        ring_wait(*p2, n)

    codes = jnp.zeros((8, LANES), jnp.float32)
    for i in range(4):
        for q in range(8):
            codes = codes + g2[i, q, blocks:blocks + 8, :]
    codes = codes.astype(jnp.int32)
    target = iota((lists, LANES), 0)

    def piece(ref, zz, yy, count):
        one = jnp.where(flat, zz, yy)
        two = jnp.where(flat, yy, zz) * 2
        return [ref[one, two, 0:count, :], ref[one, two + 1, 0:count, :]]

    def split(values):
        high = values.astype(jnp.bfloat16)
        low = (values - high.astype(jnp.float32)).astype(jnp.bfloat16)
        return jnp.concatenate([high, low], axis=1)

    def chunk(rows, values):
        slots = [(row >> 8) - 1 for row in rows]
        held = [(row & 255).astype(jnp.float32) for row in rows]
        hot = jnp.concatenate(
            [jnp.where(target == slot, 1.0, 0.0).astype(jnp.bfloat16) for slot in slots], axis=1
        )
        part = jnp.dot(hot, split(values), preferred_element_type=jnp.float32)
        held = jnp.concatenate(held, axis=1)
        held = jnp.broadcast_to(held, (LANES, held.shape[1])).astype(jnp.bfloat16)
        total = lax.dot_general(hot, held, NT, preferred_element_type=jnp.float32)
        return part[:, :LANES] + part[:, LANES:], total

    slab = jnp.zeros((lists, LANES), jnp.float32)
    totals = jnp.zeros((lists, LANES), jnp.float32)
    for zz in range(4):
        values = jnp.concatenate(sum([piece(g2, zz, yy, blocks) for yy in range(4)], []), axis=0)
        part, total = chunk([codes[2 * zz:2 * zz + 1], codes[2 * zz + 1:2 * zz + 2]], values)
        slab, totals = slab + part, totals + total
    for n in range(2, 6):
        ring_wait(*p2b, n)
    codes = jnp.zeros((8, LANES), jnp.float32)
    for i in range(4):
        for q in range(8):
            codes = codes + a2[i, q]
    codes = codes[3:5].astype(jnp.int32)
    values = jnp.concatenate(
        sum([piece(a2, zz, yy, 8) for zz in range(4) for yy in range(4)], []), axis=0
    )
    part, total = chunk([codes[0:1], codes[1:2]], values)
    slab, totals = slab + part, totals + total

    prior_load.wait()
    prior = 1.0 * PRIOR
    table[:, columns(sid)] = (
        (slab + prior * previous[...].astype(jnp.float32)) / (totals + prior)
    ).astype(jnp.bfloat16)

    def part_of(at, h):
        return table.at[pl.ds(h * (lists // 2), lists // 2), columns(core * 4 + at)]

    p3 = (along_u, u, part_of, p3_s, p3_r)
    spread = ring_start(*p3)

    def hand(n, s):
        ref = table.at[:, columns(s)]
        return copy(ref, ref, mate_s.at[n], mate_r.at[n], mate)

    order = (0, 3, 1, 2)
    relays = [hand(n, core * 4 + lax.rem(u + i, 4)) for n, i in enumerate(order)]
    relays[0].start()
    spread += ring_relay(*p3)
    ring_wait(*p3, 2)
    relays[1].start()
    ring_wait(*p3, 3)
    relays[2].start()
    ring_wait(*p3, 4)
    ring_wait(*p3, 5)
    relays[3].start()
    w = jnp.where(flat, z, y)
    for n, i in enumerate(order):
        hand(n, (1 - core) * 4 + lax.rem(w + i, 4)).wait_recv()

    ones = jnp.ones((8, table.shape[1]), jnp.bfloat16)
    squares = jnp.square(table[...].astype(jnp.float32))
    high = squares.astype(jnp.bfloat16)
    low = (squares - high.astype(jnp.float32)).astype(jnp.bfloat16)
    norms = lax.dot_general(ones, high, NT, preferred_element_type=jnp.float32)
    norms = norms + lax.dot_general(ones, low, NT, preferred_element_type=jnp.float32)
    norms_out[...] = norms
    for item in bulk[2:] + bulk_on:
        item.wait_recv()
    for j, out in enumerate((f0, f1, f2)):
        dots = lax.dot_general(arrived[j], table[...], NT, preferred_element_type=jnp.float32)
        out[...] = ((2.0 * dots - norms[0:1]) * factor).astype(jnp.bfloat16)
    for item in bulk + bulk_on + sent + sent_b + spread + relays:
        item.wait_send()


def alive_column(row):
    eye = iota((LANES, LANES), 0) == iota((LANES, LANES), 1)
    return jnp.sum(jnp.where(eye, row, 0.0), axis=1, keepdims=True)


def scores_kernel(cnt, keep, vec, table, norms, bl_hbm, hp_hbm, scores_ref, new_ref, pick_ref,
                  held, bl, hp, sems, small, *, factor, share, sizes, n_groups, n_rows):
    g = lax.axis_index("grp")
    d = lax.axis_index("row")
    tables = [
        pltpu.make_async_copy(src, dst, small.at[i])
        for i, (src, dst) in enumerate(((bl_hbm, bl), (hp_hbm, hp)))
    ]
    for item in tables:
        item.start()
    new_ref[...] = table[pl.ds(pl.multiple_of(d * share, share), share), :]
    lane = iota((1, LANES), 1)
    started, begin = [], 0
    for i, size in enumerate(sizes):
        if i >= 2:
            started[i - 2].wait()
        dots = lax.dot_general(
            vec[begin:begin + size, :], table[...], NT, preferred_element_type=jnp.float32
        )
        for b in range(size // LANES):
            k = begin // LANES + b
            row = jnp.where(lane < cnt[k], keep[k:k + 1, :], 0).astype(jnp.float32)
            held[i % 2, b * LANES:(b + 1) * LANES, :] = (
                (2.0 * dots[b * LANES:(b + 1) * LANES] - norms[0:1]) * factor
            ) * alive_column(row)
        started.append(pltpu.make_async_copy(
            held.at[i % 2, pl.ds(0, size), :], scores_ref.at[pl.ds(begin, size), :], sems.at[i % 2]
        ))
        started[-1].start()
        begin += size
    for item in tables:
        item.wait()
    blocks = keep.shape[0]
    picks = [jnp.int32(-1)] * (n_groups - 1)
    for k in range(blocks):
        home = hp[bl[(g * n_rows + d) * blocks + k]]
        away = lax.rem(home // table.shape[0] - g + n_groups, n_groups)
        picks = [jnp.where(away == j + 1, k, pick) for j, pick in enumerate(picks)]
    for j, pick in enumerate(picks):
        pick_ref[j] = pick
        pick_ref[4 + j] = jnp.maximum(pick, 0)
    for item in started[-2:]:
        item.wait()


def merge_kernel(pick, cnt, keep_ref, b0, b1, b2, _, scores_ref, held, sems):
    lane = iota((1, LANES), 1)
    backs = (b0, b1, b2)

    def put(j):
        first = pl.multiple_of(pick[4 + j] * LANES, LANES)
        return pltpu.make_async_copy(held.at[j], scores_ref.at[pl.ds(first, LANES), :], sems.at[j])

    for j, back in enumerate(backs):
        @pl.when(pick[j] >= 0)
        def _():
            k = pick[4 + j]
            row = jnp.where(lane < cnt[k], keep_ref[pl.ds(k, 1), :], 0).astype(jnp.float32)
            held[j] = back[...].astype(jnp.float32) * alive_column(row)
            put(j).start()
    for j in range(len(backs)):
        @pl.when(pick[j] >= 0)
        def _():
            put(j).wait()


def local(vectors, keep_bits, counts, block_list, home_pos, old_centroids):
    n_groups = lax.axis_size("grp")
    n_rows = lax.axis_size("row")
    blocks = counts.shape[0]
    total_rows, width = vectors.shape
    block_rows = total_rows // blocks
    lists_group = old_centroids.shape[0]
    factor = 1.0 / math.sqrt(width)
    slabs = width // LANES
    away = n_groups - 1
    keep = keep_bits.reshape(blocks, block_rows)
    whole = pl.BlockSpec(memory_space=pltpu.VMEM)
    scalars = pl.BlockSpec(memory_space=pltpu.SMEM)
    there = pl.BlockSpec(memory_space=pl.ANY)
    f32, bf16 = jnp.float32, jnp.bfloat16
    dma = pltpu.SemaphoreType.DMA
    found_shape = pltpu.VMEM((block_rows, lists_group), bf16)
    operands = (
        block_list.reshape(-1, LANES), home_pos.reshape(-1, LANES), counts.reshape(1, blocks),
        keep, vectors, old_centroids,
    )
    vec, table, norms, f0, f1, f2 = pl.pallas_call(
        functools.partial(table_kernel, n_groups=n_groups, n_rows=n_rows, factor=factor),
        out_shape=(
            pltpu.VMEM((total_rows, width), bf16),
            pltpu.VMEM((lists_group, width), bf16),
            pltpu.VMEM((8, lists_group), f32),
            found_shape, found_shape, found_shape,
        ),
        in_specs=[pl.BlockSpec(memory_space=pltpu.HBM)] * 6,
        out_specs=(whole,) * 6,
        scratch_shapes=[
            pltpu.VMEM((block_list.shape[0] // LANES, LANES), jnp.int32),
            pltpu.VMEM((home_pos.shape[0] // LANES, LANES), jnp.int32),
            pltpu.VMEM((1, blocks), jnp.int32),
            pltpu.VMEM((blocks, LANES), jnp.int32),
            pltpu.VMEM((blocks, LANES), f32),
            pltpu.VMEM((blocks, width), f32),
            pltpu.VMEM((slabs, blocks + 8, LANES), f32),
            pltpu.VMEM((away, slabs, 8, LANES), f32),
            pltpu.VMEM((away, block_rows, width), bf16),
            pltpu.VMEM((lists_group, LANES), bf16),
            pltpu.VMEM((away, slabs, 8, LANES), f32),
            pltpu.VMEM((slabs, 8, LANES), f32),
            pltpu.VMEM((4, 8, blocks + 8, LANES), f32),
            pltpu.VMEM((4, 8, 8, LANES), f32),
            pltpu.VMEM((2, block_rows // 2, width), bf16),
            pltpu.VMEM((away, block_rows, width), bf16),
            dma((8,)), dma((5,)),
            dma((8,)), dma((8,)), dma((8,)), dma((8,)),
            dma((3,)), dma((3,)), dma((6,)), dma((6,)),
            dma((6,)), dma((6,)), dma((6,)), dma((6,)), dma((6,)), dma((6,)),
            dma((4,)), dma((4,)),
        ],
        compiler_params=pltpu.CompilerParams(
            collective_id=0, has_side_effects=True, vmem_limit_bytes=24 << 20
        ),
        name="table",
    )(*(pltpu.with_memory_space_constraint(x, pltpu.HBM) for x in operands))

    backs = [
        lax.ppermute(found, "grp", [(s, (s - j - 1) % n_groups) for s in range(n_groups)])
        for j, found in enumerate((f0, f1, f2))
    ]

    sizes = [8 * block_rows] * 3 + [4 * block_rows] * 2
    scores, new_centroids, picks = pl.pallas_call(
        functools.partial(scores_kernel, factor=factor, share=lists_group // n_rows, sizes=sizes,
                          n_groups=n_groups, n_rows=n_rows),
        out_shape=(
            jax.ShapeDtypeStruct((total_rows, lists_group), f32),
            jax.ShapeDtypeStruct((lists_group // n_rows, width), bf16),
            jax.ShapeDtypeStruct((8,), jnp.int32),
        ),
        in_specs=[scalars] + [whole] * 4 + [there] * 2,
        out_specs=(there, whole, scalars),
        scratch_shapes=[
            pltpu.VMEM((2, sizes[0], lists_group), f32),
            pltpu.SMEM(block_list.shape, jnp.int32),
            pltpu.SMEM(home_pos.shape, jnp.int32),
            dma((2,)), dma((2,)),
        ],
        compiler_params=pltpu.CompilerParams(vmem_limit_bytes=24 << 20),
        cost_estimate=pl.CostEstimate(
            flops=2 * total_rows * width * lists_group,
            bytes_accessed=total_rows * 4 * lists_group,
            transcendentals=0,
        ),
        name="scores",
    )(counts, keep, vec, table, norms, block_list, home_pos)

    scores = pl.pallas_call(
        merge_kernel,
        out_shape=jax.ShapeDtypeStruct(scores.shape, f32),
        in_specs=[scalars] * 2 + [whole] * 4 + [there],
        out_specs=there,
        scratch_shapes=[pltpu.VMEM((away, block_rows, lists_group), f32), dma((away,))],
        input_output_aliases={6: 0},
        compiler_params=pltpu.CompilerParams(vmem_limit_bytes=8 << 20),
        name="merge",
    )(picks, counts, keep, *backs, scores)
    return new_centroids, scores


def solution(mesh):
    in_specs = (
        P(("grp", "row"), None),
        P(("grp", "row")),
        P(("grp", "row")),
        P(),
        P(),
        P("grp", None),
    )
    out_specs = (P(("grp", "row"), None), P(("grp", "row"), None))
    return jax.shard_map(local, mesh=mesh, in_specs=in_specs, out_specs=out_specs, check_vma=False)
```
